1024 devices in a mesh: slab: 16 (over z_hi, x), dom: 64 (over z_lo, y, core).
Axes of the slice: x: 4, y: 4, z: 32 (z_hi: 4, z_lo: 8; z = z_hi * 8 + z_lo), core: 2. Of those that a mesh axis runs over, the one named last changes fastest.
Arguments:
- positions: float32 [3, 1048576], P(None, ('slab', 'dom')), may hold values from 0 to 64, as said below
- velocities: float32 [3, 1048576], P(None, ('slab', 'dom')), may hold values from -3 to 3
- mass: float32 [1048576], P(('slab', 'dom')), may hold values from 0.005 to 0.012
- smoothing: float32 [1048576], P(('slab', 'dom')), may hold values from 0.25 to 0.4
- energy: float32 [1048576], P(('slab', 'dom')), may hold values from 0.5 to 32, as said below
- send_offsets: int32 [4, 1024], P(None, ('slab', 'dom')), may hold values from 0 to 7, as said below
- send_counts: int32 [4, 1024], P(None, ('slab', 'dom')), may hold values from 1 to 8, as said below
- pair_blocks: int32 [8, 8192], P(None, ('slab', 'dom')), may hold values from 0 to 40, as said below
Outputs:
- density: float32 [1048576], P(('slab', 'dom'))
- acceleration: float32 [3, 1048576], P(None, ('slab', 'dom'))
- heating: float32 [1048576], P(('slab', 'dom'))
- step_share: float32 [1048576], P(('slab', 'dom'))
The draws below stay inside these ranges and needn't reach their ends.
Inputs may be any that keep to these rules, and one draw needn't show every extreme that they name: `positions`: particle i of block g lies in the unit cube whose lowest corner is (slab index, domain index, local block index) of g. `energy`: largest near the middle of the box. `send_offsets`: offset plus count never passes 8. `send_counts`: some window holds all 8 blocks in every draw. `pair_blocks`: the first entry of each list is the block itself; an entry 8 (1 + r) + t names only a slot t below the count of the window received from direction r; 40 names no block; no other entry repeats within a list.
All inputs are finite; a program needn't handle non-finite values.
Results may differ from the reference program's by a relative error of at most 0.0003.
Values sent between devices are 32-bit elements; how exact they have to be, the bound alone decides.
A program may use at most 32 MiB of HBM per device.

```python
import math
import jax
import jax.numpy as jnp
from jax import lax

BLOCKS = 8
BLOCK_PTS = 128
NEIGH_BLOCKS = 8
SLABS = 16
DOMAINS = 64
DEVCOUNT = 1024
PARTICLES = 1048576


def cell_corner():
    index = jnp.arange(PARTICLES, dtype=jnp.int32)
    block = index // BLOCK_PTS
    device = block // BLOCKS
    local_block = block % BLOCKS
    return jnp.stack([device // DOMAINS, device % DOMAINS, local_block]).astype(jnp.float32)


def window_plan(key):
    base = jax.random.fold_in(key, 4242)
    key_count, key_offset = jax.random.split(base)
    counts = jax.random.randint(key_count, (4, DEVCOUNT), 1, BLOCKS + 1)
    counts = counts.at[1, 0].set(BLOCKS)
    offsets = jax.random.randint(key_offset, (4, DEVCOUNT), 0, BLOCKS - counts + 1)
    return (offsets.astype(jnp.int32), counts.astype(jnp.int32))


def draw_send_offsets(key, part):
    return window_plan(key)[0]


def draw_send_counts(key, part):
    return window_plan(key)[1]


def draw_pair_blocks(key, part):
    offsets, counts = window_plan(key)
    devices = jnp.arange(DEVCOUNT, dtype=jnp.int32)
    slab_index = devices // DOMAINS
    dom_index = devices % DOMAINS
    local = jnp.arange(BLOCKS, dtype=jnp.int32)
    peers = ((slab_index - 1, dom_index, 1, slab_index > 0), (slab_index + 1, dom_index, 0, slab_index < SLABS - 1), (slab_index, dom_index - 1, 3, dom_index > 0), (slab_index, dom_index + 1, 2, dom_index < DOMAINS - 1))
    shape = (DEVCOUNT, BLOCKS)
    own_ids = jnp.broadcast_to(local[None, :], shape)
    candidates = [(own_ids, jnp.ones(shape, bool))]
    faces = []
    edges = []
    for rank, (peer_slab, peer_dom, direction, exists) in enumerate(peers):
        peer = jnp.clip(peer_slab, 0, SLABS - 1) * DOMAINS + jnp.clip(peer_dom, 0, DOMAINS - 1)
        start = offsets[direction][peer][:, None]
        filled = counts[direction][peer][:, None]
        for shift in (0, -1, 1):
            slot = own_ids + shift - start
            valid = exists[:, None] & (slot >= 0) & (slot < filled)
            entry = (BLOCKS * (1 + rank) + slot, valid)
            if shift == 0:
                faces.append(entry)
            else:
                edges.append(entry)
    candidates = candidates + faces
    candidates.append((own_ids - 1, own_ids >= 1))
    candidates.append((own_ids + 1, own_ids < BLOCKS - 1))
    candidates = candidates + edges
    ids = jnp.stack([entry[0] for entry in candidates], axis=-1)
    valid = jnp.stack([entry[1] for entry in candidates], axis=-1)
    priority = jnp.arange(ids.shape[-1], dtype=jnp.int32)
    score = jnp.where(valid, priority, priority + 100)
    order = jnp.argsort(score, axis=-1, stable=True)[:, :, :NEIGH_BLOCKS]
    chosen = jnp.take_along_axis(ids, order, axis=-1)
    chosen_valid = jnp.take_along_axis(valid, order, axis=-1)
    result = jnp.where(chosen_valid, chosen, 5 * BLOCKS).astype(jnp.int32)
    return result.reshape(DEVCOUNT * BLOCKS, NEIGH_BLOCKS).T


def draw_positions(key, part):
    corner = cell_corner()
    base = jax.random.fold_in(key, 17)
    offset = jax.random.uniform(base, corner.shape, jnp.float32)
    return corner + offset


def draw_energy(key, part):
    corner = cell_corner()
    centre = jnp.array([SLABS / 2.0, DOMAINS / 2.0, BLOCKS / 2.0], jnp.float32)
    dist_sq = jnp.sum((corner + 0.5 - centre[:, None]) ** 2, axis=0)
    base_key = jax.random.fold_in(key, 29)
    base = jnp.exp(jax.random.uniform(base_key, (PARTICLES,), jnp.float32, jnp.log(0.5), jnp.log(2.0)))
    strength = 9.0
    return base * (1.0 + strength * jnp.exp(-dist_sq / 18.0))


def steps_of(key, dims, cuts, smallest, top_value):
    level = 1.0
    for position, blocks in cuts:
        steps = jax.random.uniform(jax.random.fold_in(jax.random.fold_in(key, 6), position), (blocks,), jnp.float32, smallest / len(cuts), top_value / len(cuts))
        level = level * jnp.repeat(jnp.exp(steps), dims[position] // blocks).reshape((-1,) + (1,) * (len(dims) - 1 - position))
    return level


def noise(key, dims, width, reach, cuts=(), kind=jnp.bfloat16):
    gain = steps_of(key, dims, cuts, -0.22, 0.18) if cuts else 1.0
    values = jax.random.normal(key, dims, jnp.float32) * width * gain
    return jnp.minimum(jnp.maximum(values, -reach), reach).astype(kind)


def setup_inputs(seed: int = 0) -> dict:
    key_of = jax.random.split(jax.random.key(seed), 9)
    positions = draw_positions(jax.random.fold_in(key_of[8], 71), 0)
    velocities = noise(key_of[1], (3, PARTICLES), 0.5, 3.0, ((1, 1024),), jnp.float32)
    mass = jnp.clip(jnp.exp(math.log(0.012) - 0.8754688 * jax.random.uniform(key_of[2], (PARTICLES,), jnp.float32) ** steps_of(key_of[2], (PARTICLES,), ((0, 1024),), -0.2, 0.2)), 0.005, 0.012)
    smoothing = jnp.clip(jnp.exp(math.log(0.4) - 0.47000364 * jax.random.uniform(key_of[3], (PARTICLES,), jnp.float32) ** steps_of(key_of[3], (PARTICLES,), ((0, 1024),), -0.2, 0.2)), 0.25, 0.4)
    energy = draw_energy(jax.random.fold_in(key_of[8], 71), 0)
    send_offsets = draw_send_offsets(jax.random.fold_in(key_of[8], 71), 0)
    send_counts = draw_send_counts(jax.random.fold_in(key_of[8], 71), 0)
    pair_blocks = draw_pair_blocks(jax.random.fold_in(key_of[8], 71), 0)
    return {"positions": positions, "velocities": velocities, "mass": mass, "smoothing": smoothing, "energy": energy, "send_offsets": send_offsets, "send_counts": send_counts, "pair_blocks": pair_blocks}


gas_gamma = 5.0 / 3.0
visc_alpha = 1.0
visc_beta = 2.0
courant = 0.4
index_pairs = ((0, 0), (1, 1), (2, 2), (0, 1), (0, 2), (1, 2))

def kernel(distance, length):
    ratio = distance / length
    shape = 0.25 * jnp.maximum(2.0 - ratio, 0.0) ** 3 - jnp.maximum(1.0 - ratio, 0.0) ** 3
    return shape / (math.pi * length ** 3)

def apply_matrix(matrix, vector):
    return jnp.stack([matrix[0] * vector[0] + matrix[3] * vector[1] + matrix[4] * vector[2], matrix[3] * vector[0] + matrix[1] * vector[1] + matrix[5] * vector[2], matrix[4] * vector[0] + matrix[5] * vector[1] + matrix[2] * vector[2]])

def block_density(pos_own, len_own, pos_near, mass_near):
    separation = pos_near[:, :, None] - pos_own[:, None, :]
    dist_sq = lax.optimization_barrier(jnp.sum(separation * separation, axis=0))
    weight = mass_near[:, None] * kernel(jnp.sqrt(dist_sq), len_own[None, :])
    dens = lax.optimization_barrier(jnp.sum(weight, axis=0))
    moments = [lax.optimization_barrier(jnp.sum(weight * separation[first] * separation[second], axis=0)) / dens for first, second in index_pairs]
    floor = 0.05 * len_own * len_own
    axx = moments[0] + floor
    ayy = moments[1] + floor
    azz = moments[2] + floor
    axy, axz, ayz = (moments[3], moments[4], moments[5])
    cof_xx = ayy * azz - ayz * ayz
    cof_yy = axx * azz - axz * axz
    cof_zz = axx * ayy - axy * axy
    cof_xy = axz * ayz - axy * azz
    cof_xz = axy * ayz - ayy * axz
    cof_yz = axy * axz - axx * ayz
    determinant = axx * cof_xx + axy * cof_xy + axz * cof_xz
    matrix = jnp.stack([cof_xx, cof_yy, cof_zz, cof_xy, cof_xz, cof_yz]) / determinant
    return (dens, matrix)

def block_momentum(own_fields, near_fields):
    separation = near_fields[0:3, :, None] - own_fields[0:3, None, :]
    dist_sq = lax.optimization_barrier(jnp.sum(separation * separation, axis=0))
    mean_len = 0.5 * (near_fields[7][:, None] + own_fields[7][None, :])
    kernel_val = kernel(jnp.sqrt(dist_sq), mean_len)
    grad_own = apply_matrix(own_fields[11:17, None, :], separation) * kernel_val
    grad_near = apply_matrix(near_fields[11:17, :, None], separation) * kernel_val
    grad_sum = grad_own + grad_near
    rel_vel = own_fields[4:7, None, :] - near_fields[4:7, :, None]
    closing = jnp.minimum(-lax.optimization_barrier(jnp.sum(rel_vel * separation, axis=0)), 0.0)
    closing_rate = mean_len * closing / (dist_sq + 0.01 * mean_len * mean_len)
    mean_sound = 0.5 * (own_fields[8][None, :] + near_fields[8][:, None])
    mean_dens = 0.5 * (own_fields[10][None, :] + near_fields[10][:, None])
    viscous = (-visc_alpha * mean_sound * closing_rate + visc_beta * closing_rate * closing_rate) / mean_dens
    near_mass = near_fields[3][:, None]
    press_own = own_fields[9][None, :]
    press_near = near_fields[9][:, None]
    acceleration = -lax.optimization_barrier(jnp.sum(near_mass * (press_own * grad_own + press_near * grad_near + 0.5 * viscous * grad_sum), axis=1))
    heating = own_fields[9] * lax.optimization_barrier(jnp.sum(near_mass * lax.optimization_barrier(jnp.sum(rel_vel * grad_own, axis=0)), axis=0))
    heating = heating + 0.25 * lax.optimization_barrier(jnp.sum(near_mass * viscous * lax.optimization_barrier(jnp.sum(rel_vel * grad_sum, axis=0)), axis=0))
    signal = lax.optimization_barrier(jnp.max(own_fields[8][None, :] + near_fields[8][:, None] - 3.0 * closing_rate, axis=0))
    return (acceleration, heating, signal)

def reference(positions, velocities, mass, smoothing, energy, send_offsets, send_counts, pair_blocks):
    total_blocks = DEVCOUNT * BLOCKS
    devices = jnp.arange(DEVCOUNT, dtype=jnp.int32)
    slab_index = devices // DOMAINS
    dom_index = devices % DOMAINS
    slots = jnp.arange(BLOCKS, dtype=jnp.int32)
    peers = ((slab_index - 1, dom_index, 1, slab_index > 0), (slab_index + 1, dom_index, 0, slab_index < SLABS - 1), (slab_index, dom_index - 1, 3, dom_index > 0), (slab_index, dom_index + 1, 2, dom_index < DOMAINS - 1))
    columns = [devices[:, None] * BLOCKS + slots[None, :]]
    for peer_slab, peer_dom, direction, exists in peers:
        peer = (jnp.clip(peer_slab, 0, SLABS - 1) * DOMAINS + jnp.clip(peer_dom, 0, DOMAINS - 1)).astype(jnp.int32)
        start = send_offsets[direction][peer]
        filled = send_counts[direction][peer]
        valid = exists[:, None] & (slots[None, :] < filled[:, None])
        columns.append(jnp.where(valid, peer[:, None] * BLOCKS + start[:, None] + slots[None, :], total_blocks).astype(jnp.int32))
    columns.append(jnp.full((DEVCOUNT, 1), total_blocks, jnp.int32))
    table_ids = jnp.concatenate(columns, axis=1)
    owner = jnp.arange(total_blocks, dtype=jnp.int32) // BLOCKS
    global_ids = table_ids[owner[None, :], pair_blocks]
    device_ids = global_ids.T.reshape(DEVCOUNT, BLOCKS, -1).astype(jnp.int32)

    def padded(fields):
        shaped = fields.reshape(fields.shape[0], total_blocks, BLOCK_PTS)
        empty = jnp.zeros((fields.shape[0], 1, BLOCK_PTS), jnp.float32)
        return jnp.concatenate([shaped, empty], axis=1)

    def per_device(fields):
        return fields.reshape(fields.shape[0], DEVCOUNT, BLOCKS, BLOCK_PTS).transpose(1, 2, 0, 3)

    def gather_near(table, ids):
        picked = table[:, ids]
        return picked.transpose(1, 0, 2, 3).reshape(ids.shape[0], table.shape[0], -1)
    table_first = padded(jnp.concatenate([positions, mass[None]], axis=0))

    def density_device(item):
        own_fields, ids = item
        near = gather_near(table_first, ids)
        return jax.vmap(block_density)(own_fields[:, 0:3], own_fields[:, 3], near[:, 0:3], near[:, 3])
    dens_parts, matrix_parts = lax.map(density_device, (per_device(jnp.concatenate([positions, smoothing[None]], axis=0)), device_ids))
    density = dens_parts.reshape(-1)
    matrices = matrix_parts.transpose(2, 0, 1, 3).reshape(6, -1)
    pressure = (gas_gamma - 1.0) * energy / density
    sound = jnp.sqrt(gas_gamma * (gas_gamma - 1.0) * energy)
    all_fields = jnp.concatenate([positions, mass[None], velocities, smoothing[None], sound[None], pressure[None], density[None], matrices], axis=0)
    table_all = padded(all_fields)

    def momentum_device(item):
        own_fields, ids = item
        near = gather_near(table_all, ids)
        return jax.vmap(block_momentum)(own_fields, near)
    accel_parts, heat_parts, signal_parts = lax.map(momentum_device, (per_device(all_fields), device_ids))
    acceleration = accel_parts.transpose(2, 0, 1, 3).reshape(3, -1)
    heating = heat_parts.reshape(-1)
    allowed = courant * smoothing / signal_parts.reshape(-1)
    step = jnp.min(allowed)
    return (density, acceleration, heating, step / allowed)
```

```python
import functools
import math

import jax
import jax.numpy as jnp
from jax import lax
from jax.experimental import pallas as pl
from jax.experimental.pallas import tpu as pltpu
from jax.sharding import PartitionSpec as P

MESH = pl.DeviceIdType.MESH
GAMMA = 5.0 / 3.0
ROWS = 32
LANES = 128
BLOCKS = 8
TABLE = 41
NEAR_Z = 5
FAR_Z = 11


def recip(x):
    r = pl.reciprocal(x, approx=True)
    return r * (2.0 - x * r)


def fold(x):
    out = x[0:8]
    for k in range(8, x.shape[0], 8):
        out = out + x[k : k + 8]
    return out


def fold_max(x):
    out = x[0:8]
    for k in range(8, x.shape[0], 8):
        out = jnp.maximum(out, x[k : k + 8])
    return out


def kernel(
    pos, vel, mass, smo, ene, offs, pairs,
    dens_o, acc_o, heat_o, share_o,
    own_a, win_a, tab_m, own_b, win_b, send_a, send_m, send_b, jt_a, jt_b, allow, best, slots,
    sa, ra, sm, rm, sb, rb, ss, sr,
):
    s, d = lax.axis_index("slab"), lax.axis_index("dom")
    zh, x, zl, y, core = s // 4, s % 4, d // 8, (d // 2) % 4, d % 2
    z = zh * 8 + zl

    def device(z, x, y, core):
        return ((z // 8) * 4 + x, (z % 8) * 8 + y * 2 + core)

    halo = [
        ((s + 15) % 16, d, s > 0),
        ((s + 1) % 16, d, s < 15),
        (s, (d + 63) % 64, d > 0),
        (s, (d + 1) % 64, d < 63),
    ]
    plane = [device(z, (x + dx) % 4, y, (core + dc) % 2) for dx in range(4) for dc in range(2) if dx or dc]
    column = [device(z, x, (y + dy) % 4, core) for dy in range(1, 4)]
    near_z = [device((z + 32 + k) % 32, x, y, core) for n in range(1, NEAR_Z + 1) for k in (n, -n)]
    edge_z = [device((z + 32 + k) % 32, x, y, core) for k in (NEAR_Z + 1, -NEAR_Z - 1)]
    far_z = [device((z + 32 + k) % 32, x, y, core) for k in (FAR_Z, -FAR_Z)]

    barrier = pltpu.get_barrier_semaphore()
    for a, b, there in halo:
        @pl.when(there)
        def _():
            pl.semaphore_signal(barrier, inc=1, device_id=(a, b), device_id_type=MESH)
    greet = plane + column + near_z + edge_z
    for peer in greet:
        pl.semaphore_signal(barrier, inc=1, device_id=peer, device_id_type=MESH)

    for b in range(BLOCKS):
        cols = slice(b * LANES, (b + 1) * LANES)
        own_a[b, 0:3] = pos[:, cols]
        own_a[b, 3:6] = vel[:, cols]
        own_a[b, 6:7] = smo[b : b + 1]
        own_a[b, 7:8] = jnp.sqrt(GAMMA * (GAMMA - 1.0) * ene[b : b + 1])
    for r in range(4):
        for t in range(BLOCKS):
            src = jnp.minimum(offs[r, 0] + t, BLOCKS - 1)
            send_a[r, t] = own_a[src]
            send_m[r, t : t + 1] = mass[pl.ds(src, 1)]

    def to_columns(b, fields, masses):
        jt_a[b] = jnp.concatenate([fields, jnp.broadcast_to(masses, (8, LANES))], axis=0).T

    def own_columns(b, carry):
        to_columns(b, own_a[b], mass[pl.ds(b, 1)])
        return carry

    lax.fori_loop(0, BLOCKS, own_columns, 0)
    jt_a[TABLE - 1] = jnp.zeros((LANES, 16), jnp.float32)
    jt_b[TABLE - 1] = jnp.zeros((LANES, 8), jnp.float32)

    waits = len(greet) + jnp.where(s > 0, 1, 0) + jnp.where(s < 15, 1, 0) + jnp.where(d > 0, 1, 0) + jnp.where(d < 63, 1, 0)
    pl.semaphore_wait(barrier, waits)

    def copy(src, dst, send, recv, peer):
        return pltpu.make_async_remote_copy(
            src_ref=src, dst_ref=dst, send_sem=send, recv_sem=recv, device_id=peer, device_id_type=MESH
        )

    def window_copies(r, back):
        a, b, _ = halo[r]
        w = r if back else r ^ 1
        first = copy(send_a.at[r], win_a.at[pl.ds(8 * w, 8)], sa.at[r], ra.at[w], (a, b))
        masses = copy(send_m.at[r], tab_m.at[w], sm.at[r], rm.at[w], (a, b))
        return first, masses

    def second_copy(r, back):
        a, b, _ = halo[r]
        w = r if back else r ^ 1
        return copy(send_b.at[r], win_b.at[pl.ds(8 * w, 8)], sb.at[r], rb.at[w], (a, b))

    for r in range(4):
        @pl.when(halo[r][2])
        def _():
            for c in window_copies(r, False):
                c.start()
    for r in (2, 3, 0, 1):
        @pl.when(halo[r][2])
        def _():
            for c in window_copies(r, True):
                c.wait_recv()

        def columns(t, carry):
            to_columns(8 * (1 + r) + t, win_a[8 * r + t], tab_m[r, pl.ds(t, 1)])
            return carry

        lax.fori_loop(0, BLOCKS, columns, 0)

    def pair_loop(g, step, carry):
        def block(k, carry):
            e = pairs[k, g]
            for r0 in range(0, LANES, ROWS):
                carry = step(e, r0, carry)
            return carry

        return lax.fori_loop(0, BLOCKS, block, carry)

    def lane_rows(g):
        own = own_a[g]
        return [own[k : k + 1] for k in range(8)]

    zero = jnp.zeros((8, LANES), jnp.float32)

    def signal_block(g, carry):
        xi, yi, zi, ui, vi, wi, hi, ci = lane_rows(g)
        hi = 0.5 * hi

        def step(e, r0, top):
            j = jt_a[e, r0 : r0 + ROWS]
            sx, sy, sz = j[:, 0:1] - xi, j[:, 1:2] - yi, j[:, 2:3] - zi
            r2 = sx * sx + sy * sy + sz * sz
            us = (j[:, 3:4] - ui) * sx + (j[:, 4:5] - vi) * sy + (j[:, 5:6] - wi) * sz
            hb = 0.5 * j[:, 6:7] + hi
            mu = hb * jnp.minimum(us, 0.0) * recip(r2 + 0.01 * hb * hb)
            return jnp.maximum(top, fold_max(j[:, 7:8] - 3.0 * mu))

        top = pair_loop(g, step, jnp.full((8, LANES), -jnp.inf))
        top = jnp.max(top, axis=0, keepdims=True) + ci
        row = 0.4 * own_a[g, 6:7] / top
        allow[pl.ds(g, 1)] = row
        return jnp.minimum(carry, row)

    low = lax.fori_loop(0, BLOCKS, signal_block, jnp.full((1, LANES), jnp.inf))
    best[...] = low

    starts = {}
    base = 0
    for name, peers in (("plane", plane), ("column", column), ("near", near_z), ("far", far_z)):
        starts[name] = (base, peers)
        base += len(peers)

    def opposite(name, k):
        return k

    def reduce_copies(name):
        first, peers = starts[name]
        return [copy(best, slots.at[first + k], ss.at[first + k], sr.at[first + k], p) for k, p in enumerate(peers)]

    def reduce_start(name):
        for c in reduce_copies(name):
            c.start()

    def reduce_end(name):
        first, peers = starts[name]
        for c in reduce_copies(name):
            c.wait()
        low = best[...]
        for k in range(len(peers)):
            low = jnp.minimum(low, slots[first + k])
        best[...] = low

    reduce_start("plane")

    def density_block(g, carry):
        xi, yi, zi, _, _, _, hi, _ = lane_rows(g)
        inv = recip(hi)

        def step(e, r0, sums):
            j = jt_a[e, r0 : r0 + ROWS]
            sx, sy, sz = j[:, 0:1] - xi, j[:, 1:2] - yi, j[:, 2:3] - zi
            r2 = sx * sx + sy * sy + sz * sz
            q = r2 * lax.rsqrt(jnp.maximum(r2, 1e-30)) * inv
            a, b = jnp.maximum(2.0 - q, 0.0), jnp.maximum(1.0 - q, 0.0)
            w = j[:, 8:9] * (0.25 * a * a * a - b * b * b)
            wx, wy, wz = w * sx, w * sy, w * sz
            parts = (w, wx * sx, wy * sy, wz * sz, wx * sy, wx * sz, wy * sz)
            return tuple(t + fold(p) for t, p in zip(sums, parts))

        sums = pair_loop(g, step, (zero,) * 7)
        sums = [jnp.sum(t, axis=0, keepdims=True) for t in sums]
        dens = sums[0] * (inv * inv * inv * (1.0 / math.pi))
        per = 1.0 / sums[0]
        floor = 0.05 * hi * hi
        axx, ayy, azz = [t * per + floor for t in sums[1:4]]
        axy, axz, ayz = [t * per for t in sums[4:7]]
        cxx = ayy * azz - ayz * ayz
        cyy = axx * azz - axz * axz
        czz = axx * ayy - axy * axy
        cxy = axz * ayz - axy * azz
        cxz = axy * ayz - ayy * axz
        cyz = axy * axz - axx * ayz
        det = 1.0 / (axx * cxx + axy * cxy + axz * cxz)
        own_b[g, 0:1] = dens
        for k, v in enumerate((cxx, cyy, czz, cxy, cxz, cyz)):
            own_b[g, 1 + k : 2 + k] = v * det
        own_b[g, 7:8] = (GAMMA - 1.0) * ene[pl.ds(g, 1)] / dens
        dens_o[pl.ds(g, 1)] = dens
        jt_b[g] = own_b[g].T

        @pl.when(g == 1)
        def _():
            reduce_end("plane")
            reduce_start("column")

        @pl.when(g == 4)
        def _():
            reduce_end("column")
            reduce_start("near")

        return carry

    lax.fori_loop(0, BLOCKS, density_block, 0)

    for r in range(4):
        for t in range(BLOCKS):
            send_b[r, t] = own_b[jnp.minimum(offs[r, 0] + t, BLOCKS - 1)]
    for r in range(4):
        @pl.when(halo[r][2])
        def _():
            second_copy(r, False).start()
    reduce_end("near")
    reduce_start("far")
    for r in (2, 3, 0, 1):
        @pl.when(halo[r][2])
        def _():
            second_copy(r, True).wait_recv()

        def columns(t, carry):
            jt_b[8 * (1 + r) + t] = win_b[8 * r + t].T
            return carry

        lax.fori_loop(0, BLOCKS, columns, 0)

    def momentum_block(g, carry):
        xi, yi, zi, ui, vi, wi, hi, ci = lane_rows(g)
        hi, ci = 0.5 * hi, 0.5 * ci
        own = own_b[g]
        ri = 0.5 * own[0:1]
        cxx, cyy, czz, cxy, cxz, cyz, pi = [own[k : k + 1] for k in range(1, 8)]

        def step(e, r0, sums):
            j, k = jt_a[e, r0 : r0 + ROWS], jt_b[e, r0 : r0 + ROWS]
            sx, sy, sz = j[:, 0:1] - xi, j[:, 1:2] - yi, j[:, 2:3] - zi
            r2 = sx * sx + sy * sy + sz * sz
            ux, uy, uz = ui - j[:, 3:4], vi - j[:, 4:5], wi - j[:, 5:6]
            us = ux * sx + uy * sy + uz * sz
            hb = 0.5 * j[:, 6:7] + hi
            inv = recip(hb)
            q = r2 * lax.rsqrt(jnp.maximum(r2, 1e-30)) * inv
            a, b = jnp.maximum(2.0 - q, 0.0), jnp.maximum(1.0 - q, 0.0)
            w = (1.0 / math.pi) * j[:, 8:9] * (0.25 * a * a * a - b * b * b) * (inv * inv * inv)
            mu = hb * jnp.minimum(-us, 0.0) * recip(r2 + 0.01 * hb * hb)
            cb = 0.5 * j[:, 7:8] + ci
            half = 0.5 * w * mu * (2.0 * mu - cb) * recip(0.5 * k[:, 0:1] + ri)
            dxx, dyy, dzz, dxy, dxz, dyz = [k[:, n : n + 1] for n in range(1, 7)]
            tx = dxx * sx + dxy * sy + dxz * sz
            ty = dxy * sx + dyy * sy + dyz * sz
            tz = dxz * sx + dyz * sy + dzz * sz
            ox = cxx * sx + cxy * sy + cxz * sz
            oy = cxy * sx + cyy * sy + cyz * sz
            oz = cxz * sx + cyz * sy + czz * sz
            wp = w * pi
            one, two = wp + half, w * k[:, 7:8] + half
            parts = (
                one * ox + two * tx,
                one * oy + two * ty,
                one * oz + two * tz,
                (wp + 0.5 * half) * (ux * ox + uy * oy + uz * oz) + 0.5 * half * (ux * tx + uy * ty + uz * tz),
            )
            return tuple(t + fold(p) for t, p in zip(sums, parts))

        sums = pair_loop(g, step, (zero,) * 4)
        sums = [jnp.sum(t, axis=0, keepdims=True) for t in sums]
        cols = pl.ds(pl.multiple_of(g * LANES, LANES), LANES)
        for k in range(3):
            acc_o[k : k + 1, cols] = -sums[k]
        heat_o[pl.ds(g, 1)] = sums[3]
        return carry

    lax.fori_loop(0, BLOCKS, momentum_block, 0)

    reduce_end("far")
    share_o[...] = jnp.min(best[...], axis=1, keepdims=True) / allow[...]

    for r in range(4):
        @pl.when(halo[r][2])
        def _():
            for c in window_copies(r, False):
                c.wait_send()
            second_copy(r, False).wait_send()


def body(positions, velocities, mass, smoothing, energy, send_offsets, send_counts, pair_blocks):
    tile = (BLOCKS, LANES)
    vmem, smem = pl.BlockSpec(memory_space=pltpu.VMEM), pl.BlockSpec(memory_space=pltpu.SMEM)
    f32 = jnp.float32
    dma = pltpu.SemaphoreType.DMA
    n_slots = 7 + 3 + 2 * NEAR_Z + 2
    dens, acc, heat, share = pl.pallas_call(
        kernel,
        out_shape=(
            jax.ShapeDtypeStruct(tile, f32),
            jax.ShapeDtypeStruct(positions.shape, f32),
            jax.ShapeDtypeStruct(tile, f32),
            jax.ShapeDtypeStruct(tile, f32),
        ),
        in_specs=[vmem] * 5 + [smem] * 2,
        out_specs=(vmem,) * 4,
        scratch_shapes=[
            pltpu.VMEM((8, 8, LANES), f32),
            pltpu.VMEM((32, 8, LANES), f32),
            pltpu.VMEM((4, 8, LANES), f32),
            pltpu.VMEM((8, 8, LANES), f32),
            pltpu.VMEM((32, 8, LANES), f32),
            pltpu.VMEM((4, 8, 8, LANES), f32),
            pltpu.VMEM((4, 8, LANES), f32),
            pltpu.VMEM((4, 8, 8, LANES), f32),
            pltpu.VMEM((TABLE, LANES, 16), f32),
            pltpu.VMEM((TABLE, LANES, 8), f32),
            pltpu.VMEM(tile, f32),
            pltpu.VMEM((1, LANES), f32),
            pltpu.VMEM((n_slots, 1, LANES), f32),
            dma((4,)), dma((4,)), dma((4,)), dma((4,)), dma((4,)), dma((4,)),
            dma((n_slots,)), dma((n_slots,)),
        ],
        compiler_params=pltpu.CompilerParams(collective_id=0, has_side_effects=True),
        name="sph",
    )(
        positions, velocities, mass.reshape(tile), smoothing.reshape(tile), energy.reshape(tile),
        send_offsets, pair_blocks,
    )
    return dens.reshape(-1), acc, heat.reshape(-1), share.reshape(-1)


def solution(mesh):
    many = P(None, ("slab", "dom"))
    flat = P(("slab", "dom"))
    return jax.shard_map(
        body,
        mesh=mesh,
        in_specs=(many, many, flat, flat, flat, many, many, many),
        out_specs=(flat, many, flat, flat),
        check_vma=False,
    )
```

```python
import functools
import math

import jax
import jax.numpy as jnp
from jax import lax
from jax.experimental import pallas as pl
from jax.experimental.pallas import tpu as pltpu
from jax.sharding import PartitionSpec as P

MESH = pl.DeviceIdType.MESH
GAMMA = 5.0 / 3.0
CHUNK = 4
UNROLL = 8
PARTS = 4
LANES = 128
BLOCKS = 8
TABLE = 41
NEAR_Z = 5
FAR_Z = 11


def recip(x):
    r = pl.reciprocal(x, approx=True)
    return r * (2.0 - x * r)


def kernel(
    pos, vel, mass, smo, ene, offs, pairs,
    dens_o, acc_o, heat_o, share_o,
    own_a, win_a, tab_m, own_b, win_b, send_a, send_m, send_b, near_a, near_b, self_a, self_b, kept, early, tile, allow, best, slots,
    sa, ra, sm, rm, sb, rb, ss, sr,
):
    s, d = lax.axis_index("slab"), lax.axis_index("dom")
    zh, x, zl, y, core = s // 4, s % 4, d // 8, (d // 2) % 4, d % 2
    z = zh * 8 + zl

    def device(z, x, y, core):
        return ((z // 8) * 4 + x, (z % 8) * 8 + y * 2 + core)

    halo = [
        ((s + 15) % 16, d, s > 0),
        ((s + 1) % 16, d, s < 15),
        (s, (d + 63) % 64, d > 0),
        (s, (d + 1) % 64, d < 63),
    ]
    plane = [device(z, (x + dx) % 4, y, (core + dc) % 2) for dx in range(4) for dc in range(2) if dx or dc]
    column = [device(z, x, (y + dy) % 4, core) for dy in range(1, 4)]
    near_z = [device((z + 32 + k) % 32, x, y, core) for n in range(1, NEAR_Z + 1) for k in (n, -n)]
    edge_z = [device((z + 32 + k) % 32, x, y, core) for k in (NEAR_Z + 1, -NEAR_Z - 1)]
    far_z = [device((z + 32 + k) % 32, x, y, core) for k in (FAR_Z, -FAR_Z)]

    barrier = pltpu.get_barrier_semaphore()
    for a, b, there in halo:
        @pl.when(there)
        def _():
            pl.semaphore_signal(barrier, inc=1, device_id=(a, b), device_id_type=MESH)
    greet = plane + column + near_z + edge_z
    for peer in greet:
        pl.semaphore_signal(barrier, inc=1, device_id=peer, device_id_type=MESH)

    for b in range(BLOCKS):
        cols = slice(b * LANES, (b + 1) * LANES)
        own_a[b, 0:3] = pos[:, cols]
        own_a[b, 3:6] = vel[:, cols]
        own_a[b, 6:7] = 0.5 * smo[b : b + 1]
        own_a[b, 7:8] = 0.5 * jnp.sqrt(GAMMA * (GAMMA - 1.0) * ene[b : b + 1])
    for r in range(4):
        for t in range(BLOCKS):
            src = jnp.minimum(offs[r, 0] + t, BLOCKS - 1)
            send_a[r, t] = own_a[src]
            send_m[r, t : t + 1] = mass[pl.ds(src, 1)]

    def spread_first(b, fields, masses):
        for f in range(8):
            near_a[b, f] = jnp.broadcast_to(fields[f : f + 1], (8, LANES))
        near_a[b, 8] = jnp.broadcast_to(masses, (8, LANES))

    def spread_second(b, fields):
        for f in range(8):
            near_b[b, f] = jnp.broadcast_to(fields[f : f + 1], (8, LANES))

    def across(rows, f):
        return jnp.broadcast_to(rows[:, f : f + 1], (LANES, LANES)).reshape(16, 8, LANES)

    def own_first(b, carry):
        fields = own_a[b]
        spread_first(b, fields, mass[pl.ds(b, 1)])
        columns = fields.T
        for f in range(8):
            self_a[b, f] = across(columns, f)
        self_a[b, 8] = across(recip(2.0 * columns[:, 6:7]), 0)
        return carry

    lax.fori_loop(0, BLOCKS, own_first, 0)
    near_a[TABLE - 1] = jnp.zeros((9, 8, LANES), jnp.float32)
    near_b[TABLE - 1] = jnp.zeros((8, 8, LANES), jnp.float32)
    lane = lax.broadcasted_iota(jnp.int32, (CHUNK, 8, LANES), 2)

    waits = len(greet) + jnp.where(s > 0, 1, 0) + jnp.where(s < 15, 1, 0) + jnp.where(d > 0, 1, 0) + jnp.where(d < 63, 1, 0)
    pl.semaphore_wait(barrier, waits)

    def copy(src, dst, send, recv, peer):
        return pltpu.make_async_remote_copy(
            src_ref=src, dst_ref=dst, send_sem=send, recv_sem=recv, device_id=peer, device_id_type=MESH
        )

    def window_copies(r, back):
        a, b, _ = halo[r]
        w = r if back else r ^ 1
        first = copy(send_a.at[r], win_a.at[pl.ds(8 * w, 8)], sa.at[r], ra.at[w], (a, b))
        masses = copy(send_m.at[r], tab_m.at[w], sm.at[r], rm.at[w], (a, b))
        return first, masses

    def second_copy(r, back):
        a, b, _ = halo[r]
        w = r if back else r ^ 1
        return copy(send_b.at[r], win_b.at[pl.ds(8 * w, 8)], sb.at[r], rb.at[w], (a, b))

    for r in range(4):
        @pl.when(halo[r][2])
        def _():
            for c in window_copies(r, False):
                c.start()
    for r in (2, 3, 0, 1):
        @pl.when(halo[r][2])
        def _():
            for c in window_copies(r, True):
                c.wait_recv()

        def arrived(t, carry):
            spread_first(8 * (1 + r) + t, win_a[8 * r + t], tab_m[r, pl.ds(t, 1)])
            return carry

        lax.fori_loop(0, BLOCKS, arrived, 0)

    def pair_sums(g, count, start, make, collect):
        def part(at):
            step = make(at)

            def block(k, sums):
                for i in range(UNROLL):
                    sums = step(pairs[k * UNROLL + i, g], k * UNROLL + i, sums)
                return sums

            zero = jnp.full((CHUNK, 8, LANES), start, jnp.float32)
            sums = lax.fori_loop(0, BLOCKS // UNROLL, block, (zero,) * count)
            out = jnp.zeros((CHUNK, 8, LANES), jnp.float32)
            for q, t in enumerate(sums):
                out = jnp.where(lane == q, collect(t, axis=2, keepdims=True), out)
            tile[at] = out

        def chunk(n, carry):
            for i in range(PARTS):
                part(pl.ds((n * PARTS + i) * CHUNK, CHUNK))
            return carry

        lax.fori_loop(0, 16 // (PARTS * CHUNK), chunk, 0)
        rows = tile[...].reshape(LANES, LANES).T
        return [rows[q : q + 1] for q in range(count)]

    def signal_block(g, carry):
        def make(at):
            def step(e, k, sums):
                sx, sy, sz = [near_a[e, f] - self_a[g, f, at] for f in range(3)]
                ux, uy, uz = [near_a[e, f] - self_a[g, f, at] for f in range(3, 6)]
                r2 = sx * sx + sy * sy + sz * sz
                us = ux * sx + uy * sy + uz * sz
                hb = near_a[e, 6] + self_a[g, 6, at]
                mu = hb * jnp.minimum(us, 0.0) * recip(r2 + 0.01 * hb * hb)
                kept[g, k, 0, at] = r2
                kept[g, k, 1, at] = mu
                return (jnp.maximum(sums[0], near_a[e, 7] - 1.5 * mu),)

            return step

        (top,) = pair_sums(g, 1, -jnp.inf, make, jnp.max)
        row = 0.4 * own_a[g, 6:7] / (top + own_a[g, 7:8])
        allow[pl.ds(g, 1)] = row
        return jnp.minimum(carry, row)

    low = lax.fori_loop(0, BLOCKS, signal_block, jnp.full((1, LANES), jnp.inf))
    best[...] = low

    starts = {}
    base = 0
    for name, peers in (("plane", plane), ("column", column), ("near", near_z), ("far", far_z)):
        starts[name] = (base, peers)
        base += len(peers)

    def opposite(name, k):
        return k

    def reduce_copies(name):
        first, peers = starts[name]
        return [copy(best, slots.at[first + k], ss.at[first + k], sr.at[first + k], p) for k, p in enumerate(peers)]

    def reduce_start(name):
        for c in reduce_copies(name):
            c.start()

    def reduce_end(name):
        first, peers = starts[name]
        for c in reduce_copies(name):
            c.wait()
        low = best[...]
        for k in range(len(peers)):
            low = jnp.minimum(low, slots[first + k])
        best[...] = low

    reduce_start("plane")

    def density_block(g, carry):
        hi = 2.0 * own_a[g, 6:7]
        inv = recip(hi)
        def make(at):
            def step(e, k, sums):
                sx, sy, sz = [near_a[e, f] - self_a[g, f, at] for f in range(3)]
                r2 = kept[g, k, 0, at]
                q = r2 * lax.rsqrt(jnp.maximum(r2, 1e-30)) * self_a[g, 8, at]
                a, b = jnp.maximum(2.0 - q, 0.0), jnp.maximum(1.0 - q, 0.0)
                w = near_a[e, 8] * (0.25 * a * a * a - b * b * b)
                wx, wy, wz = w * sx, w * sy, w * sz
                parts = (w, wx * sx, wy * sy, wz * sz, wx * sy, wx * sz, wy * sz)
                return tuple(t + p for t, p in zip(sums, parts))

            return step

        sums = pair_sums(g, 7, 0.0, make, jnp.sum)
        dens = sums[0] * (inv * inv * inv * (1.0 / math.pi))
        per = 1.0 / sums[0]
        floor = 0.05 * hi * hi
        axx, ayy, azz = [t * per + floor for t in sums[1:4]]
        axy, axz, ayz = [t * per for t in sums[4:7]]
        cxx = ayy * azz - ayz * ayz
        cyy = axx * azz - axz * axz
        czz = axx * ayy - axy * axy
        cxy = axz * ayz - axy * azz
        cxz = axy * ayz - ayy * axz
        cyz = axy * axz - axx * ayz
        det = 1.0 / (axx * cxx + axy * cxy + axz * cxz)
        own_b[g, 0:1] = dens
        for k, v in enumerate((cxx, cyy, czz, cxy, cxz, cyz)):
            own_b[g, 1 + k : 2 + k] = v * det
        own_b[g, 7:8] = (GAMMA - 1.0) * ene[pl.ds(g, 1)] / dens
        dens_o[pl.ds(g, 1)] = dens
        spread_second(g, own_b[g])

        @pl.when(g == 2)
        def _():
            reduce_end("plane")
            reduce_start("column")

        @pl.when(g == 5)
        def _():
            reduce_end("column")
            reduce_start("near")

        return carry

    lax.fori_loop(0, BLOCKS, density_block, 0)

    for r in range(4):
        for t in range(BLOCKS):
            send_b[r, t] = own_b[jnp.minimum(offs[r, 0] + t, BLOCKS - 1)]
    for r in range(4):
        @pl.when(halo[r][2])
        def _():
            second_copy(r, False).start()

    def early_block(g, carry):
        columns = own_b[g].T
        for f in range(7):
            self_b[g, f] = across(columns, f)

        def make(at):
            def step(e, k, sums):
                sx, sy, sz = [near_a[e, f] - self_a[g, f, at] for f in range(3)]
                ux, uy, uz = [near_a[e, f] - self_a[g, f, at] for f in range(3, 6)]
                r2, mu = kept[g, k, 0, at], kept[g, k, 1, at]
                hb = near_a[e, 6] + self_a[g, 6, at]
                inv = recip(hb)
                q = r2 * lax.rsqrt(jnp.maximum(r2, 1e-30)) * inv
                a, b = jnp.maximum(2.0 - q, 0.0), jnp.maximum(1.0 - q, 0.0)
                w = near_a[e, 8] * (0.25 * a * a * a - b * b * b) * (inv * inv * inv)
                cb = near_a[e, 7] + self_a[g, 7, at]
                cxx, cyy, czz, cxy, cxz, cyz = [self_b[g, f, at] for f in range(1, 7)]
                ox = cxx * sx + cxy * sy + cxz * sz
                oy = cxy * sx + cyy * sy + cyz * sz
                oz = cxz * sx + cyz * sy + czz * sz
                uo = ux * ox + uy * oy + uz * oz
                kept[g, k, 0, at] = w
                kept[g, k, 1, at] = w * mu * (2.0 * mu - cb)
                kept[g, k, 2, at] = uo
                return tuple(t + p for t, p in zip(sums, (w * sx, w * sy, w * sz, w * uo)))

            return step

        for q, row in enumerate(pair_sums(g, 4, 0.0, make, jnp.sum)):
            early[g, q : q + 1] = row

        @pl.when(g == 1)
        def _():
            reduce_end("near")
            reduce_start("far")

        return carry

    lax.fori_loop(0, BLOCKS, early_block, 0)
    for r in (2, 3, 0, 1):
        @pl.when(halo[r][2])
        def _():
            second_copy(r, True).wait_recv()

        def arrived(t, carry):
            spread_second(8 * (1 + r) + t, win_b[8 * r + t])
            return carry

        lax.fori_loop(0, BLOCKS, arrived, 0)

    def momentum_block(g, carry):
        def make(at):
            def step(e, k, sums):
                sx, sy, sz = [near_a[e, f] - self_a[g, f, at] for f in range(3)]
                ux, uy, uz = [near_a[e, f] - self_a[g, f, at] for f in range(3, 6)]
                w, viscous, uo = [kept[g, k, n, at] for n in range(3)]
                half = viscous * recip(near_b[e, 0] + self_b[g, 0, at])
                dxx, dyy, dzz, dxy, dxz, dyz = [near_b[e, f] for f in range(1, 7)]
                tx = dxx * sx + dxy * sy + dxz * sz
                ty = dxy * sx + dyy * sy + dyz * sz
                tz = dxz * sx + dyz * sy + dzz * sz
                two = w * near_b[e, 7] + half
                work = uo + (ux * tx + uy * ty + uz * tz)
                parts = (two * tx, two * ty, two * tz, half * sx, half * sy, half * sz, half * work)
                return tuple(t + p for t, p in zip(sums, parts))

            return step

        late = pair_sums(g, 7, 0.0, make, jnp.sum)
        own = own_b[g]
        cxx, cyy, czz, cxy, cxz, cyz, pi = [own[f : f + 1] for f in range(1, 8)]
        px, py, pz, pw = [pi * early[g, q : q + 1] for q in range(4)]
        px, py, pz = px + late[3], py + late[4], pz + late[5]
        sums = [
            cxx * px + cxy * py + cxz * pz + late[0],
            cxy * px + cyy * py + cyz * pz + late[1],
            cxz * px + cyz * py + czz * pz + late[2],
            -pw - 0.5 * late[6],
        ]
        sums = [t * (1.0 / math.pi) for t in sums]
        cols = pl.ds(pl.multiple_of(g * LANES, LANES), LANES)
        for k in range(3):
            acc_o[k : k + 1, cols] = -sums[k]
        heat_o[pl.ds(g, 1)] = sums[3]
        return carry

    lax.fori_loop(0, BLOCKS, momentum_block, 0)

    reduce_end("far")
    share_o[...] = jnp.min(best[...], axis=1, keepdims=True) / allow[...]

    for r in range(4):
        @pl.when(halo[r][2])
        def _():
            for c in window_copies(r, False):
                c.wait_send()
            second_copy(r, False).wait_send()


def body(positions, velocities, mass, smoothing, energy, send_offsets, send_counts, pair_blocks):
    shape = (BLOCKS, LANES)
    vmem, smem = pl.BlockSpec(memory_space=pltpu.VMEM), pl.BlockSpec(memory_space=pltpu.SMEM)
    f32 = jnp.float32
    dma = pltpu.SemaphoreType.DMA
    n_slots = 7 + 3 + 2 * NEAR_Z + 2
    dens, acc, heat, share = pl.pallas_call(
        kernel,
        out_shape=(
            jax.ShapeDtypeStruct(shape, f32),
            jax.ShapeDtypeStruct(positions.shape, f32),
            jax.ShapeDtypeStruct(shape, f32),
            jax.ShapeDtypeStruct(shape, f32),
        ),
        in_specs=[vmem] * 5 + [smem] * 2,
        out_specs=(vmem,) * 4,
        scratch_shapes=[
            pltpu.VMEM((8, 8, LANES), f32),
            pltpu.VMEM((32, 8, LANES), f32),
            pltpu.VMEM((4, 8, LANES), f32),
            pltpu.VMEM((8, 8, LANES), f32),
            pltpu.VMEM((32, 8, LANES), f32),
            pltpu.VMEM((4, 8, 8, LANES), f32),
            pltpu.VMEM((4, 8, LANES), f32),
            pltpu.VMEM((4, 8, 8, LANES), f32),
            pltpu.VMEM((TABLE, 9, 8, LANES), f32),
            pltpu.VMEM((TABLE, 8, 8, LANES), f32),
            pltpu.VMEM((BLOCKS, 9, 16, 8, LANES), f32),
            pltpu.VMEM((BLOCKS, 7, 16, 8, LANES), f32),
            pltpu.VMEM((BLOCKS, BLOCKS, 3, 16, 8, LANES), f32),
            pltpu.VMEM((BLOCKS, 8, LANES), f32),
            pltpu.VMEM((16, 8, LANES), f32),
            pltpu.VMEM(shape, f32),
            pltpu.VMEM((1, LANES), f32),
            pltpu.VMEM((n_slots, 1, LANES), f32),
            dma((4,)), dma((4,)), dma((4,)), dma((4,)), dma((4,)), dma((4,)),
            dma((n_slots,)), dma((n_slots,)),
        ],
        compiler_params=pltpu.CompilerParams(collective_id=0, has_side_effects=True),
        name="sph",
    )(
        positions, velocities, mass.reshape(shape), smoothing.reshape(shape), energy.reshape(shape),
        send_offsets, pair_blocks,
    )
    return dens.reshape(-1), acc, heat.reshape(-1), share.reshape(-1)


def solution(mesh):
    many = P(None, ("slab", "dom"))
    flat = P(("slab", "dom"))
    return jax.shard_map(
        body,
        mesh=mesh,
        in_specs=(many, many, flat, flat, flat, many, many, many),
        out_specs=(flat, many, flat, flat),
        check_vma=False,
    )
```
